128 devices in a mesh: row: 16 (over z, y_hi, core), col: 8 (over y_lo, x).
Axes of the slice: x: 4, y: 4 (y_hi: 2, y_lo: 2; y = y_hi * 2 + y_lo), z: 4, core: 2. Of those that a mesh axis runs over, the one named last changes fastest.
Arguments:
- sky_image: bfloat16 [2, 16384, 16384], P(None, 'row', 'col'), may hold values from -6 to 6
- facet_rows: int32 [128], replicated, may hold values from 512 to 15872
- facet_offsets: int32 [128], replicated, may hold values from 0 to 127
- facet_owner: int32 [128], replicated, may hold values from 0 to 127, each once
Outputs:
- facets: bfloat16 [128, 2, 1024, 1024], P(('row', 'col'))
The draws below stay inside these ranges and needn't reach their ends.
Inputs may be any that keep to these rules, and one draw needn't show every extreme that they name: `facet_owner`: the entries are distinct, so every device owns exactly one facet.
All inputs are finite; a program needn't handle non-finite values.
Results may differ from the reference program's by a relative error of at most 0.0095.
Values may be sent and summed in bfloat16 or wider, within the bound.
No kernel may reach another device: no remote copies, remote signals or barrier semaphores. Data moves between devices by JAX's collectives and lax.ppermute only.
A program may use at most 128 MiB of HBM per device.

```python
import math
import jax
import jax.numpy as jnp
from jax import lax

N = 16384
FS = 1024
SPLIT = 128
BLOCKS = 128
STRIP = 128
LEAD = 128
FACETS = 128


def plant(drawn, own_key, low, high):
    longest = drawn.shape.index(max(drawn.shape))
    spots = []
    for shift in (0, 1):
        where = [jax.random.randint(jax.random.fold_in(own_key, axis), (), 0, length) for axis, length in enumerate(drawn.shape)]
        where[longest] = (where[longest] + shift) % drawn.shape[longest]
        spots.append(tuple(where))
    return drawn.at[spots[0]].set(low).at[spots[1]].set(high)


def level_of(key, dims, split, low, largest):
    loudness = 1.0
    for position, parts in split:
        draws = jax.random.uniform(jax.random.fold_in(jax.random.fold_in(key, 6), position), (parts,), jnp.float32, low / len(split), largest / len(split))
        loudness = loudness * jnp.repeat(jnp.exp(draws), dims[position] // parts).reshape((-1,) + (1,) * (len(dims) - 1 - position))
    return loudness


def centred(rng, dims, scale, most, shards=(), kind=jnp.bfloat16):
    result = scale * jax.random.normal(rng, dims, jnp.float32)
    if shards:
        result = result * level_of(rng, dims, shards, -0.22, 0.18)
    return jnp.clip(result, -most, most).astype(kind)


def setup_inputs(seed: int = 0) -> dict:
    streams_of = jax.random.split(jax.random.key(seed), 5)
    sky_image = centred(streams_of[0], (2, N, N), 1.0, 6.0, ((1, 16), (2, 8)))
    facet_rows = plant(jax.random.randint(streams_of[1], (FACETS,), FS // 2, N - FS // 2 + 1), jax.random.fold_in(streams_of[1], 1), FS // 2, (N - FS // 2 + 1) - 1).astype(jnp.int32)
    facet_offsets = plant(jax.random.randint(streams_of[2], (FACETS,), 0, STRIP), jax.random.fold_in(streams_of[2], 1), 0, STRIP - 1).astype(jnp.int32)
    facet_owner = jax.random.permutation(streams_of[3], BLOCKS).astype(jnp.int32)
    return dict(sky_image=sky_image, facet_rows=facet_rows, facet_offsets=facet_offsets, facet_owner=facet_owner)


def dft_table(length):
    positions = jnp.arange(length, dtype=jnp.int32)
    turn_count = positions[:, None] * positions[None, :] % length
    angles = turn_count.astype(jnp.float32) * (-2.0 * math.pi / length)
    factor = 1.0 / math.sqrt(length)
    return ((jnp.cos(angles) * factor).astype(jnp.bfloat16), (jnp.sin(angles) * factor).astype(jnp.bfloat16))

def twiddle_table(first_len, second_len, total):
    left_index = jnp.arange(first_len, dtype=jnp.int32)[:, None]
    right_index = jnp.arange(second_len, dtype=jnp.int32)[None, :]
    angles = (left_index * right_index % total).astype(jnp.float32) * (-2.0 * math.pi / total)
    return (jnp.cos(angles), jnp.sin(angles))

def complex_mix(formula, tables, values):
    tab_re = tables[0].astype(jnp.float32)
    tab_im = tables[1].astype(jnp.float32)
    val_re = values[0].astype(jnp.float32)
    val_im = values[1].astype(jnp.float32)
    re_part = jnp.einsum(formula, tab_re, val_re) - jnp.einsum(formula, tab_im, val_im)
    im_part = jnp.einsum(formula, tab_re, val_im) + jnp.einsum(formula, tab_im, val_re)
    return (re_part, im_part)

def rotate(pair, twiddle):
    return (pair[0] * twiddle[0] - pair[1] * twiddle[1], pair[0] * twiddle[1] + pair[1] * twiddle[0])

def as_stored(pair):
    return jnp.stack((pair[0].astype(jnp.bfloat16), pair[1].astype(jnp.bfloat16)))

def rows_pass(strip_rows):
    blocks = strip_rows.reshape(2, STRIP, LEAD, SPLIT)
    mixed_pair = complex_mix('pa,rab->rpb', dft_table(LEAD), (blocks[0], blocks[1]))
    section_one = as_stored(rotate(mixed_pair, twiddle_table(LEAD, SPLIT, N)))
    mixed_pair = complex_mix('qb,rpb->rqp', dft_table(SPLIT), (section_one[0], section_one[1]))
    return as_stored(mixed_pair).reshape(2, STRIP, N)

def columns_pass(strip_cols):
    grouped = strip_cols.reshape(2, BLOCKS, STRIP, STRIP)
    mixed_pair = complex_mix('pg,gic->pic', dft_table(BLOCKS), (grouped[0], grouped[1]))
    twiddle = twiddle_table(BLOCKS, STRIP, N)
    section_two = as_stored(rotate(mixed_pair, (twiddle[0][:, :, None], twiddle[1][:, :, None])))
    mixed_pair = complex_mix('qi,pic->qpc', dft_table(STRIP), (section_two[0], section_two[1]))
    return as_stored(mixed_pair).reshape(2, N, STRIP)

def reference(sky_image, facet_rows, facet_offsets, facet_owner):
    row_blocks = jnp.moveaxis(sky_image.reshape(2, BLOCKS, STRIP, N), 1, 0)
    done_blocks = lax.map(rows_pass, row_blocks)
    rows_done = jnp.moveaxis(done_blocks, 0, 1).reshape(2, N, N)
    col_blocks = jnp.moveaxis(rows_done.reshape(2, N, BLOCKS, STRIP), 2, 0)
    grid_blocks = lax.map(columns_pass, col_blocks)
    grid_full = jnp.moveaxis(grid_blocks, 0, 2).reshape(2, N, N)
    device_ids = jnp.arange(BLOCKS, dtype=jnp.int32)
    matches = (facet_owner[None, :] == device_ids[:, None]).astype(jnp.int32)
    owned_count = lax.optimization_barrier(jnp.sum(matches, axis=1))
    centre_row = jnp.where(owned_count > 0, lax.optimization_barrier(jnp.sum(matches * facet_rows[None, :], axis=1)), FS // 2)
    centre_col = lax.optimization_barrier(jnp.sum(matches * facet_offsets[None, :], axis=1))
    taper_axis = 0.25 + 0.75 * jnp.sin(math.pi * (jnp.arange(FS, dtype=jnp.float32) + 0.5) / FS)

    def cut_facet(packed):
        device, row_at, col_at, owned = packed
        start_row = (row_at - FS // 2).astype(jnp.int32)
        band_rows = lax.dynamic_slice_in_dim(grid_full, start_row, FS, 1)
        col_index = ((device * STRIP + col_at - FS // 2 + jnp.arange(FS, dtype=jnp.int32)) % N).astype(jnp.int32)
        tile = jnp.take(band_rows, col_index, axis=2)
        weight = taper_axis[:, None] * taper_axis[None, :] * owned.astype(jnp.float32)
        return (tile.astype(jnp.float32) * weight).astype(jnp.bfloat16)
    return lax.map(cut_facet, (device_ids, centre_row, centre_col, owned_count))
```

```python
import math

import jax
import jax.numpy as jnp
import numpy as np
from jax import lax
from jax.experimental import pallas as pl
from jax.experimental.pallas import tpu as pltpu
from jax.sharding import PartitionSpec as P

N = 16384
FS = 1024
L = 128
REACH = 4
CHUNKS = 2
MIB = 1 << 20


def dft_parts():
    k = np.arange(L)
    angles = (k[:, None] * k[None, :] % L) * (-2.0 * math.pi / L)
    scale = 1.0 / math.sqrt(L)
    return np.cos(angles) * scale, np.sin(angles) * scale


def twiddles():
    k = np.arange(L)
    angles = (k[:, None] * k[None, :] % N) * (-2.0 * math.pi / N)
    return np.stack((np.cos(angles), np.sin(angles))).astype(np.float32)


def real_form(order):
    re, im = dft_parts()
    plane = np.array([o[0] for o in order])
    index = np.array([o[1] for o in order])
    top = np.where(plane[None, :] == 0, re[:, index], -im[:, index])
    low = np.where(plane[None, :] == 0, im[:, index], re[:, index])
    return jnp.asarray(np.concatenate((top, low)), jnp.bfloat16)


def in_hbm(array):
    return pltpu.with_memory_space_constraint(array, pltpu.HBM)


def params(limit):
    return pltpu.CompilerParams(vmem_limit_bytes=limit * MIB)


def pack_body(x_ref, out_ref, scr):
    rows = x_ref.shape[1]
    for plane in range(2):
        for a in range(16):
            scr[pl.ds((plane * 16 + a) * rows, rows), :] = x_ref[plane, :, a * L : (a + 1) * L].astype(jnp.float32)
    for r in range(rows):
        for plane in range(2):
            out_ref[0, r, plane] = scr[pl.ds(plane * 16 * rows + r, 16, stride=rows), :].astype(jnp.bfloat16)


def pack(image, chunk, rows):
    step = 32
    per = rows // step
    peers = image.shape[1] // L
    return pl.pallas_call(
        pack_body,
        name="pack",
        grid=(peers, per),
        in_specs=[pl.BlockSpec((2, step, 2048), lambda c, j: (0, c * (L // step) + chunk * per + j, 0))],
        out_specs=pl.BlockSpec((1, step, 2, 16, L), lambda c, j: (c, j, 0, 0, 0)),
        out_shape=pltpu.HBM((peers, rows, 2, 16, L), jnp.bfloat16),
        scratch_shapes=[pltpu.VMEM((2 * 16 * step, L), jnp.float32)],
        compiler_params=params(24),
    )(in_hbm(image))


def rows_body(x_ref, g_ref, h_ref, tw_ref, out_ref, scr):
    for pair in range(8):
        data = jnp.concatenate([x_ref[:, 2 * pair + e].reshape(2 * L, L) for e in range(2)], axis=1)
        mixed = jnp.dot(g_ref[...], data, preferred_element_type=jnp.float32)
        turned = []
        for e in range(2):
            re = mixed[:L, e * L : (e + 1) * L]
            im = mixed[L:, e * L : (e + 1) * L]
            turned.append(
                jnp.concatenate(
                    (
                        (re * tw_ref[0] - im * tw_ref[1]).astype(jnp.bfloat16),
                        (re * tw_ref[1] + im * tw_ref[0]).astype(jnp.bfloat16),
                    ),
                    axis=1,
                )
            )
        section = jnp.concatenate(turned, axis=0)
        done = lax.dot_general(h_ref[...], section, (((1,), (1,)), ((), ())), preferred_element_type=jnp.float32)
        for e in range(2):
            scr[pl.ds((2 * pair + e) * 2 * L, 2 * L), :] = done[:, e * L : (e + 1) * L]
    for plane in range(2):
        for q in range(L):
            out_ref[q, plane] = scr[pl.ds(plane * L + q, 16, stride=2 * L), :].astype(jnp.bfloat16)


def rows_pass(x, g, h, tw):
    peers, rows = x.shape[:2]
    whole = lambda j: (0, 0)
    return pl.pallas_call(
        rows_body,
        name="rows_pass",
        grid=(rows // 16,),
        in_specs=[
            pl.BlockSpec((peers, 16, 2, 16, L), lambda j: (0, j, 0, 0, 0)),
            pl.BlockSpec((2 * L, 2 * L), whole),
            pl.BlockSpec((2 * L, 2 * L), whole),
            pl.BlockSpec((2, L, L), lambda j: (0, 0, 0)),
        ],
        out_specs=pl.BlockSpec((L, 2, 16, L), lambda j: (0, 0, j, 0)),
        out_shape=pltpu.HBM((L, 2, rows, L), jnp.bfloat16),
        scratch_shapes=[pltpu.VMEM((16 * 2 * L, L), jnp.float32)],
        compiler_params=params(32),
    )(in_hbm(x), g, h, tw)


def columns_body(x_ref, g_ref, tw_ref, out_ref, scr, scr2):
    scr[...] = x_ref[...].reshape(2 * L * 16, L).astype(jnp.float32)
    for pair in range(8):
        data = jnp.concatenate(
            [scr[pl.ds(2 * pair + e, 2 * L, stride=16), :].astype(jnp.bfloat16) for e in range(2)], axis=1
        )
        mixed = jnp.dot(g_ref[...], data, preferred_element_type=jnp.float32)
        for e in range(2):
            i = 2 * pair + e
            re = mixed[:L, e * L : (e + 1) * L]
            im = mixed[L:, e * L : (e + 1) * L]
            t_re = jnp.broadcast_to(tw_ref[0, 0, :, i : i + 1], (L, L))
            t_im = jnp.broadcast_to(tw_ref[0, 1, :, i : i + 1], (L, L))
            scr2[pl.ds(i * 2 * L, L), :] = re * t_re - im * t_im
            scr2[pl.ds(i * 2 * L + L, L), :] = re * t_im + im * t_re
    for plane in range(2):
        for p in range(L):
            out_ref[p, plane] = scr2[pl.ds(plane * L + p, 16, stride=2 * L), :].astype(jnp.bfloat16)


def columns_pass(x, g, tw, chunk):
    rows = x.shape[2]
    blocks = rows // 16
    return pl.pallas_call(
        columns_body,
        name="columns_pass",
        grid=(blocks,),
        in_specs=[
            pl.BlockSpec((L, 2, 16, L), lambda j: (0, 0, j, 0)),
            pl.BlockSpec((2 * L, 2 * L), lambda j: (0, 0)),
            pl.BlockSpec((1, 2, L, 16), lambda j: (chunk * blocks + j, 0, 0, 0)),
        ],
        out_specs=pl.BlockSpec((L, 2, 16, L), lambda j: (0, 0, j, 0)),
        out_shape=pltpu.HBM((L, 2, rows, L), jnp.bfloat16),
        scratch_shapes=[pltpu.VMEM((2 * L * 16, L), jnp.float32), pltpu.VMEM((16 * 2 * L, L), jnp.float32)],
        compiler_params=params(32),
    )(in_hbm(x), g, tw)


STEPS = 8


def bands_body(starts_ref, *refs):
    x_refs, f_ref, outs, scr = refs[:CHUNKS], refs[CHUNKS], refs[CHUNKS + 1 : -1], refs[-1]
    step = pl.program_id(0)
    per = L // STEPS

    def transformed(p):
        data = jnp.concatenate([x_ref[p, plane] for x_ref in x_refs for plane in range(2)], axis=0)
        return jnp.dot(f_ref[...], data, preferred_element_type=jnp.float32)

    @pl.when(step < STEPS)
    def _():
        for p in range(per):
            base = pl.multiple_of((step * per + p) * 2 * L, 2 * L)
            scr[pl.ds(base, 2 * L), :] = transformed(p)

    @pl.when(step == 0)
    def _():
        for p in range(16):
            scr[pl.ds((L + p) * 2 * L, 2 * L), :] = scr[pl.ds(p * 2 * L + 1, 2 * L), :]

    @pl.when(step == STEPS - 1)
    def _():
        for slot, out_ref in enumerate(outs):
            first = starts_ref[slot]
            top = first // L
            shift = first % L
            for group in range(L // 16):
                p = shift + 16 * group
                wrapped = (p >= L).astype(jnp.int32)
                base = (p - L * wrapped) * 2 * L + top + wrapped
                for plane in range(2):
                    for u in range(FS // L):
                        tile = scr[pl.ds(base + plane * L + u, 16, stride=2 * L), :]
                        out_ref[plane, u * L + 16 * group : u * L + 16 * group + 16, :] = tile.astype(jnp.bfloat16)


def bands(parts, table, starts):
    targets = starts.shape[0]
    rows = parts[0].shape[2]
    per = L // STEPS
    return pl.pallas_call(
        bands_body,
        name="bands",
        grid_spec=pltpu.PrefetchScalarGridSpec(
            num_scalar_prefetch=1,
            grid=(STEPS,),
            in_specs=[
                pl.BlockSpec((per, 2, rows, L), lambda j, s: (j, 0, 0, 0)) for _ in parts
            ]
            + [pl.BlockSpec((2 * L, 2 * L), lambda j, s: (0, 0))],
            out_specs=[pl.BlockSpec((2, FS, L), lambda j, s: (0, 0, 0))] * targets,
            scratch_shapes=[pltpu.VMEM(((L + 16) * 2 * L, L), jnp.float32)],
        ),
        out_shape=[jax.ShapeDtypeStruct((2, FS, L), jnp.bfloat16)] * targets,
        compiler_params=params(40),
    )(starts, *map(in_hbm, parts), table)


def facet_body(scal_ref, *refs):
    strips, down_ref, across_ref, out_ref = refs[: 2 * REACH + 1], refs[-3], refs[-2], refs[-1]
    shift = scal_ref[0]
    rows = out_ref.shape[2]
    owned = scal_ref[1].astype(jnp.float32)
    down = jnp.broadcast_to(down_ref[...], (rows, L))
    keep = lax.broadcasted_iota(jnp.int32, (rows, L), 1) < L - shift
    back = lax.rem(L - shift, L)
    for plane in range(2):
        turned = [pltpu.roll(s[plane].astype(jnp.float32), back, 1) for s in strips]
        for j in range(FS // L):
            tile = jnp.where(keep, turned[j], turned[j + 1])
            weight = down * across_ref[:, j * L : (j + 1) * L] * owned
            out_ref[0, plane, :, j * L : (j + 1) * L] = (tile * weight).astype(jnp.bfloat16)


def facet(strips, scalars):
    rows = 128
    taper = (0.25 + 0.75 * np.sin(math.pi * (np.arange(FS) + 0.5) / FS)).astype(np.float32)
    return pl.pallas_call(
        facet_body,
        name="facet",
        grid_spec=pltpu.PrefetchScalarGridSpec(
            num_scalar_prefetch=1,
            grid=(FS // rows,),
            in_specs=[pl.BlockSpec((2, rows, L), lambda j, s: (0, j, 0)) for _ in strips]
            + [pl.BlockSpec((rows, 1), lambda j, s: (j, 0)), pl.BlockSpec((1, FS), lambda j, s: (0, 0))],
            out_specs=pl.BlockSpec((1, 2, rows, FS), lambda j, s: (0, 0, j, 0)),
        ),
        out_shape=jax.ShapeDtypeStruct((1, 2, FS, FS), jnp.bfloat16),
        compiler_params=params(32),
    )(scalars, *strips, jnp.asarray(taper[:, None]), jnp.asarray(taper[None, :]))


def shifted(block, axis, distance):
    devices = range(lax.axis_size(axis))
    route = [((i - distance) % len(devices), i) for i in devices]
    return lax.ppermute(block, axis, route)


def shards(sky_image, facet_rows, facet_offsets, facet_owner):
    both = ("row", "col")
    devices = lax.axis_size(both)
    rows = L // CHUNKS
    first_rows = real_form([(plane, 16 * c + a) for c in range(8) for plane in range(2) for a in range(16)])
    second_rows = real_form([(plane, b) for plane in range(2) for b in range(L)])
    first_cols = real_form([(plane, s) for s in range(L) for plane in range(2)])
    second_cols = real_form(
        [(plane, h * rows + i) for h in range(CHUNKS) for plane in range(2) for i in range(rows)]
    )
    turn = twiddles()
    turn_cols = turn.reshape(2, L, 8, 16).transpose(2, 0, 1, 3)

    my_index = lax.axis_index(both)
    targets = (my_index + jnp.arange(REACH, -REACH - 1, -1, dtype=jnp.int32)) % devices
    matches = (facet_owner[None, :] == targets[:, None]).astype(jnp.int32)
    owned = jnp.sum(matches, axis=1)
    starts = jnp.where(owned > 0, jnp.sum(matches * facet_rows[None, :], axis=1) - FS // 2, 0)
    offset = jnp.sum(matches[REACH] * facet_offsets)
    scalars = jnp.stack((offset, owned[REACH]))

    parts = []
    for chunk in range(CHUNKS):
        sent = pack(sky_image, chunk, rows)
        strip = lax.all_to_all(sent, "col", split_axis=0, concat_axis=0, tiled=True)
        done = rows_pass(strip, first_rows, second_rows, jnp.asarray(turn))
        columns = lax.all_to_all(done, both, split_axis=0, concat_axis=0, tiled=True)
        parts.append(columns_pass(columns, first_cols, jnp.asarray(turn_cols), chunk))
    cut = bands(parts, second_cols, starts)
    strips = []
    for slot, distance in enumerate(range(REACH, -REACH - 1, -1)):
        strips.append(cut[slot] if distance == 0 else shifted(cut[slot], both, distance))
    return facet(strips, scalars)


def solution(mesh):
    placed = (P(None, "row", "col"), P(), P(), P())
    return jax.shard_map(
        shards,
        mesh=mesh,
        in_specs=placed,
        out_specs=P(("row", "col"), None, None, None),
        check_vma=False,
    )
```

```python
import math

import jax
import jax.numpy as jnp
import numpy as np
from jax import lax
from jax.experimental import pallas as pl
from jax.experimental.pallas import tpu as pltpu
from jax.sharding import PartitionSpec as P

N = 16384
FS = 1024
L = 128
REACH = 4
CHUNKS = 1
MIB = 1 << 20
PITCH = 2 * L + 4


def dft_parts():
    k = np.arange(L)
    angles = (k[:, None] * k[None, :] % L) * (-2.0 * math.pi / L)
    scale = 1.0 / math.sqrt(L)
    return np.cos(angles) * scale, np.sin(angles) * scale


def twiddles():
    k = np.arange(L)
    angles = (k[:, None] * k[None, :] % N) * (-2.0 * math.pi / N)
    return np.stack((np.cos(angles), np.sin(angles))).astype(np.float32)


def real_form(order):
    re, im = dft_parts()
    plane = np.array([o[0] for o in order])
    index = np.array([o[1] for o in order])
    top = np.where(plane[None, :] == 0, re[:, index], -im[:, index])
    low = np.where(plane[None, :] == 0, im[:, index], re[:, index])
    return jnp.asarray(np.concatenate((top, low)), jnp.bfloat16)


def in_hbm(array):
    return pltpu.with_memory_space_constraint(array, pltpu.HBM)


def params(limit):
    return pltpu.CompilerParams(vmem_limit_bytes=limit * MIB)


def pack_body(x_ref, out_ref):
    rows = x_ref.shape[1]
    for plane in range(2):
        for r in range(0, rows, 16):
            out_ref[0, r : r + 16, plane] = x_ref[plane, r : r + 16, :].reshape(16, 16, L)


def pack(image, chunk, rows):
    step = 64
    per = rows // step
    peers = image.shape[1] // L
    return pl.pallas_call(
        pack_body,
        name="pack",
        grid=(peers, per),
        in_specs=[pl.BlockSpec((2, step, 2048), lambda c, j: (0, c * (L // step) + chunk * per + j, 0))],
        out_specs=pl.BlockSpec((1, step, 2, 16, L), lambda c, j: (c, j, 0, 0, 0)),
        out_shape=pltpu.HBM((peers, rows, 2, 16, L), jnp.bfloat16),
        compiler_params=params(24),
    )(in_hbm(image))


def rows_body(x_ref, g_ref, h_ref, tw_ref, out_ref, scr):
    for pair in range(8):
        data = jnp.concatenate([x_ref[:, 2 * pair + e].reshape(2 * L, L) for e in range(2)], axis=1)
        mixed = jnp.dot(g_ref[...], data, preferred_element_type=jnp.float32)
        turned = []
        for e in range(2):
            re = mixed[:L, e * L : (e + 1) * L]
            im = mixed[L:, e * L : (e + 1) * L]
            turned.append(
                jnp.concatenate(
                    (
                        (re * tw_ref[0] - im * tw_ref[1]).astype(jnp.bfloat16),
                        (re * tw_ref[1] + im * tw_ref[0]).astype(jnp.bfloat16),
                    ),
                    axis=1,
                )
            )
        section = jnp.concatenate(turned, axis=0)
        done = lax.dot_general(h_ref[...], section, (((1,), (1,)), ((), ())), preferred_element_type=jnp.float32)
        for e in range(2):
            scr[pl.ds((2 * pair + e) * PITCH, 2 * L), :] = done[:, e * L : (e + 1) * L]
    for plane in range(2):
        for q in range(L):
            out_ref[q, plane] = scr[pl.ds(plane * L + q, 16, stride=PITCH), :].astype(jnp.bfloat16)


def rows_pass(x, g, h, tw):
    peers, rows = x.shape[:2]
    whole = lambda j: (0, 0)
    return pl.pallas_call(
        rows_body,
        name="rows_pass",
        grid=(rows // 16,),
        in_specs=[
            pl.BlockSpec((peers, 16, 2, 16, L), lambda j: (0, j, 0, 0, 0)),
            pl.BlockSpec((2 * L, 2 * L), whole),
            pl.BlockSpec((2 * L, 2 * L), whole),
            pl.BlockSpec((2, L, L), lambda j: (0, 0, 0)),
        ],
        out_specs=pl.BlockSpec((L, 2, 16, L), lambda j: (0, 0, j, 0)),
        out_shape=pltpu.HBM((L, 2, rows, L), jnp.bfloat16),
        scratch_shapes=[pltpu.VMEM((16 * PITCH, L), jnp.float32)],
        compiler_params=params(32),
    )(in_hbm(x), g, h, tw)


def columns_body(x_ref, g_ref, tw_ref, out_ref, scr, scr2):
    for s in range(0, L, 8):
        scr[:, 2 * s : 2 * s + 16, :] = jnp.swapaxes(x_ref[s : s + 8].reshape(16, 16, L), 0, 1)
    for pair in range(8):
        data = jnp.concatenate([scr[2 * pair + e] for e in range(2)], axis=1)
        mixed = jnp.dot(g_ref[...], data, preferred_element_type=jnp.float32)
        for e in range(2):
            i = 2 * pair + e
            re = mixed[:L, e * L : (e + 1) * L]
            im = mixed[L:, e * L : (e + 1) * L]
            t_re = jnp.broadcast_to(tw_ref[0, 0, :, i : i + 1], (L, L))
            t_im = jnp.broadcast_to(tw_ref[0, 1, :, i : i + 1], (L, L))
            scr2[pl.ds(i * PITCH, L), :] = re * t_re - im * t_im
            scr2[pl.ds(i * PITCH + L, L), :] = re * t_im + im * t_re
    for plane in range(2):
        for p in range(L):
            out_ref[p, plane] = scr2[pl.ds(plane * L + p, 16, stride=PITCH), :].astype(jnp.bfloat16)


def columns_pass(x, g, tw, chunk):
    rows = x.shape[2]
    blocks = rows // 16
    return pl.pallas_call(
        columns_body,
        name="columns_pass",
        grid=(blocks,),
        in_specs=[
            pl.BlockSpec((L, 2, 16, L), lambda j: (0, 0, j, 0)),
            pl.BlockSpec((2 * L, 2 * L), lambda j: (0, 0)),
            pl.BlockSpec((1, 2, L, 16), lambda j: (chunk * blocks + j, 0, 0, 0)),
        ],
        out_specs=pl.BlockSpec((L, 2, 16, L), lambda j: (0, 0, j, 0)),
        out_shape=pltpu.HBM((L, 2, rows, L), jnp.bfloat16),
        scratch_shapes=[pltpu.VMEM((16, 2 * L, L), jnp.bfloat16), pltpu.VMEM((16 * PITCH, L), jnp.float32)],
        compiler_params=params(32),
    )(in_hbm(x), g, tw)


STEPS = 8


def bands_body(starts_ref, *refs):
    x_refs, f_ref, outs, scr = refs[:CHUNKS], refs[CHUNKS], refs[CHUNKS + 1 : -1], refs[-1]
    step = pl.program_id(0)
    per = L // STEPS

    def transformed(p):
        data = jnp.concatenate([x_ref[p, plane] for x_ref in x_refs for plane in range(2)], axis=0)
        return jnp.dot(f_ref[...], data, preferred_element_type=jnp.float32)

    @pl.when(step < STEPS)
    def _():
        for p in range(per):
            scr[pl.ds((step * per + p) * PITCH, 2 * L), :] = transformed(p)

    @pl.when(step == 0)
    def _():
        for p in range(16):
            scr[pl.ds((L + p) * PITCH, 2 * L), :] = scr[pl.ds(p * PITCH + 1, 2 * L), :]

    @pl.when(step == STEPS - 1)
    def _():
        for slot, out_ref in enumerate(outs):
            first = starts_ref[slot]
            top = first // L
            shift = first % L
            for group in range(L // 16):
                p = shift + 16 * group
                wrapped = (p >= L).astype(jnp.int32)
                base = (p - L * wrapped) * PITCH + top + wrapped
                for plane in range(2):
                    for u in range(FS // L):
                        tile = scr[pl.ds(base + plane * L + u, 16, stride=PITCH), :]
                        out_ref[plane, u * L + 16 * group : u * L + 16 * group + 16, :] = tile.astype(jnp.bfloat16)


def bands(parts, table, starts):
    targets = starts.shape[0]
    rows = parts[0].shape[2]
    per = L // STEPS
    return pl.pallas_call(
        bands_body,
        name="bands",
        grid_spec=pltpu.PrefetchScalarGridSpec(
            num_scalar_prefetch=1,
            grid=(STEPS,),
            in_specs=[
                pl.BlockSpec((per, 2, rows, L), lambda j, s: (j, 0, 0, 0)) for _ in parts
            ]
            + [pl.BlockSpec((2 * L, 2 * L), lambda j, s: (0, 0))],
            out_specs=[pl.BlockSpec((2, FS, L), lambda j, s: (0, 0, 0))] * targets,
            scratch_shapes=[pltpu.VMEM(((L + 16) * PITCH, L), jnp.float32)],
        ),
        out_shape=[jax.ShapeDtypeStruct((2, FS, L), jnp.bfloat16)] * targets,
        compiler_params=params(40),
    )(starts, *map(in_hbm, parts), table)


def facet_body(scal_ref, *refs):
    strips, down_ref, across_ref, out_ref = refs[: 2 * REACH + 1], refs[-3], refs[-2], refs[-1]
    shift = scal_ref[0]
    rows = out_ref.shape[2]
    owned = scal_ref[1].astype(jnp.float32)
    down = jnp.broadcast_to(down_ref[...], (rows, L))
    keep = lax.broadcasted_iota(jnp.int32, (rows, L), 1) < L - shift
    back = lax.rem(L - shift, L)
    for plane in range(2):
        turned = [pltpu.roll(s[plane].astype(jnp.float32), back, 1) for s in strips]
        for j in range(FS // L):
            tile = jnp.where(keep, turned[j], turned[j + 1])
            weight = down * across_ref[:, j * L : (j + 1) * L] * owned
            out_ref[0, plane, :, j * L : (j + 1) * L] = (tile * weight).astype(jnp.bfloat16)


def facet(strips, scalars):
    rows = 128
    taper = (0.25 + 0.75 * np.sin(math.pi * (np.arange(FS) + 0.5) / FS)).astype(np.float32)
    return pl.pallas_call(
        facet_body,
        name="facet",
        grid_spec=pltpu.PrefetchScalarGridSpec(
            num_scalar_prefetch=1,
            grid=(FS // rows,),
            in_specs=[pl.BlockSpec((2, rows, L), lambda j, s: (0, j, 0)) for _ in strips]
            + [pl.BlockSpec((rows, 1), lambda j, s: (j, 0)), pl.BlockSpec((1, FS), lambda j, s: (0, 0))],
            out_specs=pl.BlockSpec((1, 2, rows, FS), lambda j, s: (0, 0, j, 0)),
        ),
        out_shape=jax.ShapeDtypeStruct((1, 2, FS, FS), jnp.bfloat16),
        compiler_params=params(32),
    )(scalars, *strips, jnp.asarray(taper[:, None]), jnp.asarray(taper[None, :]))


def shifted(block, axis, distance):
    devices = range(lax.axis_size(axis))
    route = [((i - distance) % len(devices), i) for i in devices]
    return lax.ppermute(block, axis, route)


def shards(sky_image, facet_rows, facet_offsets, facet_owner):
    both = ("row", "col")
    devices = lax.axis_size(both)
    rows = L // CHUNKS
    first_rows = real_form([(plane, 16 * c + a) for c in range(8) for plane in range(2) for a in range(16)])
    second_rows = real_form([(plane, b) for plane in range(2) for b in range(L)])
    first_cols = real_form([(plane, s) for s in range(L) for plane in range(2)])
    second_cols = real_form(
        [(plane, h * rows + i) for h in range(CHUNKS) for plane in range(2) for i in range(rows)]
    )
    turn = twiddles()
    turn_cols = turn.reshape(2, L, 8, 16).transpose(2, 0, 1, 3)

    my_index = lax.axis_index(both)
    targets = (my_index + jnp.arange(REACH, -REACH - 1, -1, dtype=jnp.int32)) % devices
    matches = (facet_owner[None, :] == targets[:, None]).astype(jnp.int32)
    owned = jnp.sum(matches, axis=1)
    starts = jnp.where(owned > 0, jnp.sum(matches * facet_rows[None, :], axis=1) - FS // 2, 0)
    offset = jnp.sum(matches[REACH] * facet_offsets)
    scalars = jnp.stack((offset, owned[REACH]))

    parts = []
    for chunk in range(CHUNKS):
        sent = pack(sky_image, chunk, rows)
        strip = lax.all_to_all(sent, "col", split_axis=0, concat_axis=0, tiled=True)
        done = rows_pass(strip, first_rows, second_rows, jnp.asarray(turn))
        columns = lax.all_to_all(done, both, split_axis=0, concat_axis=0, tiled=True)
        parts.append(columns_pass(columns, first_cols, jnp.asarray(turn_cols), chunk))
    cut = bands(parts, second_cols, starts)
    strips = []
    for slot, distance in enumerate(range(REACH, -REACH - 1, -1)):
        strips.append(cut[slot] if distance == 0 else shifted(cut[slot], both, distance))
    return facet(strips, scalars)


def solution(mesh):
    placed = (P(None, "row", "col"), P(), P(), P())
    return jax.shard_map(
        shards,
        mesh=mesh,
        in_specs=placed,
        out_specs=P(("row", "col"), None, None, None),
        check_vma=False,
    )
```

```python
import math
from functools import partial

import jax
import jax.numpy as jnp
import numpy as np
from jax import lax
from jax.experimental import pallas as pl
from jax.experimental.pallas import tpu as pltpu
from jax.sharding import PartitionSpec as P

N = 16384
FS = 1024
L = 128
REACH = 4
MIB = 1 << 20
PITCH = 2 * L + 4
ROW_GROUPS = 2


def dft_parts():
    k = np.arange(L)
    angles = (k[:, None] * k[None, :] % L) * (-2.0 * math.pi / L)
    scale = 1.0 / math.sqrt(L)
    return np.cos(angles) * scale, np.sin(angles) * scale


def twiddles():
    k = np.arange(L)
    angles = (k[:, None] * k[None, :] % N) * (-2.0 * math.pi / N)
    return np.stack((np.cos(angles), np.sin(angles))).astype(np.float32)


def real_form(order):
    re, im = dft_parts()
    plane = np.array([o[0] for o in order])
    index = np.array([o[1] for o in order])
    top = np.where(plane[None, :] == 0, re[:, index], -im[:, index])
    low = np.where(plane[None, :] == 0, im[:, index], re[:, index])
    return jnp.asarray(np.concatenate((top, low)), jnp.bfloat16)


def in_hbm(array):
    return pltpu.with_memory_space_constraint(array, pltpu.HBM)


def params(limit):
    return pltpu.CompilerParams(vmem_limit_bytes=limit * MIB)


PACK_ROWS = 64
AHEAD = 4


def pack_body(x_ref, out_ref, taken, given, scr, in_sems, out_sems):
    slices = x_ref.shape[1] // PACK_ROWS

    def fetch(k):
        return pltpu.make_async_copy(x_ref.at[:, pl.ds(k * PACK_ROWS, PACK_ROWS), :], taken.at[k], in_sems.at[k])

    def store(k):
        return pltpu.make_async_copy(given.at[k], out_ref.at[pl.ds(k * PACK_ROWS, PACK_ROWS)], out_sems.at[k])

    for k in range(AHEAD):
        fetch(k).start()

    def one(k, carry):
        fetch(k).wait()

        @pl.when(k + AHEAD < slices)
        def _():
            fetch(k + AHEAD).start()

        for plane in range(2):
            for a in range(16):
                scr[pl.ds((plane * 16 + a) * 68, PACK_ROWS), :] = taken[k, plane, :, a * L : (a + 1) * L].astype(
                    jnp.float32
                )
            for i in range(PACK_ROWS):
                given[k, i, plane] = scr[pl.ds(plane * 16 * 68 + i, 16, stride=68), :].astype(jnp.bfloat16)
        store(k).start()
        return carry

    lax.fori_loop(0, slices, one, 0)

    def drain(k, carry):
        store(k).wait()
        return carry

    lax.fori_loop(0, slices, drain, 0)


def pack(image):
    rows = image.shape[1]
    slices = rows // PACK_ROWS
    return pl.pallas_call(
        pack_body,
        name="pack",
        in_specs=[pl.BlockSpec(memory_space=pl.ANY)],
        out_specs=pl.BlockSpec(memory_space=pl.ANY),
        out_shape=pltpu.HBM((rows, 2, 16, L), jnp.bfloat16),
        scratch_shapes=[
            pltpu.VMEM((slices, 2, PACK_ROWS, 16 * L), jnp.bfloat16),
            pltpu.VMEM((slices, PACK_ROWS, 2, 16, L), jnp.bfloat16),
            pltpu.VMEM((2 * 16 * 68, L), jnp.float32),
            pltpu.SemaphoreType.DMA((slices,)),
            pltpu.SemaphoreType.DMA((slices,)),
        ],
        compiler_params=params(32),
    )(in_hbm(image))


def rows_body(x_ref, g_ref, h_ref, tw_ref, out_ref, scr):
    for group in range(ROW_GROUPS):
        base = group * 16 * PITCH
        for pair in range(8):
            data = jnp.concatenate([x_ref[:, group * 16 + 2 * pair + e].reshape(2 * L, L) for e in range(2)], axis=1)
            mixed = jnp.dot(g_ref[...], data, preferred_element_type=jnp.float32)
            turned = []
            for e in range(2):
                re = mixed[:L, e * L : (e + 1) * L]
                im = mixed[L:, e * L : (e + 1) * L]
                turned.append(
                    jnp.concatenate(
                        (
                            (re * tw_ref[0] - im * tw_ref[1]).astype(jnp.bfloat16),
                            (re * tw_ref[1] + im * tw_ref[0]).astype(jnp.bfloat16),
                        ),
                        axis=1,
                    )
                )
            section = jnp.concatenate(turned, axis=0)
            done = lax.dot_general(h_ref[...], section, (((1,), (1,)), ((), ())), preferred_element_type=jnp.float32)
            for e in range(2):
                scr[pl.ds(base + (2 * pair + e) * PITCH, 2 * L), :] = done[:, e * L : (e + 1) * L]
        for plane in range(2):
            for q in range(L):
                tile = scr[pl.ds(base + plane * L + q, 16, stride=PITCH), :]
                out_ref[q, plane, group * 16 : group * 16 + 16, :] = tile.astype(jnp.bfloat16)


def rows_pass(x, g, h, tw):
    peers, rows = x.shape[:2]
    whole = lambda j: (0, 0)
    return pl.pallas_call(
        rows_body,
        name="rows_pass",
        grid=(rows // (16 * ROW_GROUPS),),
        in_specs=[
            pl.BlockSpec((peers, 16 * ROW_GROUPS, 2, 16, L), lambda j: (0, j, 0, 0, 0)),
            pl.BlockSpec((2 * L, 2 * L), whole),
            pl.BlockSpec((2 * L, 2 * L), whole),
            pl.BlockSpec((2, L, L), lambda j: (0, 0, 0)),
        ],
        out_specs=pl.BlockSpec((L, 2, 16 * ROW_GROUPS, L), lambda j: (0, 0, j, 0)),
        out_shape=pltpu.HBM((L, 2, rows, L), jnp.bfloat16),
        scratch_shapes=[pltpu.VMEM((ROW_GROUPS * 16 * PITCH, L), jnp.float32)],
        compiler_params=params(32),
    )(in_hbm(x), g, h, tw)


STEPS = 4
BANDS = 8


def columns_body(starts_ref, x_ref, g_ref, tw_ref, f_ref, *refs):
    outs = refs[:-6]
    spreads, turns = refs[-6:-4], refs[-4:-2]
    section, grid = refs[-2:]
    step = pl.program_id(0)
    per = L // BANDS

    @pl.when(step < STEPS)
    def _():
        for group, (spread, turned) in enumerate(zip(spreads, turns)):
            rows = pl.ds(pl.multiple_of(step * 32 + group * 16, 16), 16)
            for k in range(2 * L):
                tile = x_ref[k // 2, k % 2, group * 16 : group * 16 + 16]
                spread[pl.ds(k * 20, 16), :] = tile.astype(jnp.float32)
            for pair in range(8):
                data = jnp.concatenate(
                    [spread[pl.ds(2 * pair + e, 2 * L, stride=20), :].astype(jnp.bfloat16) for e in range(2)], axis=1
                )
                mixed = jnp.dot(g_ref[...], data, preferred_element_type=jnp.float32)
                for e in range(2):
                    i = 2 * pair + e
                    re = mixed[:L, e * L : (e + 1) * L]
                    im = mixed[L:, e * L : (e + 1) * L]
                    at = group * 16 + i
                    t_re = jnp.broadcast_to(tw_ref[0, 0, :, at : at + 1], (L, L))
                    t_im = jnp.broadcast_to(tw_ref[0, 1, :, at : at + 1], (L, L))
                    turned[pl.ds(i * PITCH, L), :] = re * t_re - im * t_im
                    turned[pl.ds(i * PITCH + L, L), :] = re * t_im + im * t_re
            for plane in range(2):
                for p in range(L):
                    tile = turned[pl.ds(plane * L + p, 16, stride=PITCH), :]
                    section[p, plane, rows, :] = tile.astype(jnp.bfloat16)

    @pl.when(step >= STEPS)
    def _():
        for pair in range(per // 2):
            p = (step - STEPS) * per + 2 * pair
            data = jnp.concatenate([section[p + e].reshape(2 * L, L) for e in range(2)], axis=1)
            done = jnp.dot(f_ref[...], data, preferred_element_type=jnp.float32)
            for e in range(2):
                grid[pl.ds((p + e) * PITCH, 2 * L), :] = done[:, e * L : (e + 1) * L]

    @pl.when(step == STEPS)
    def _():
        for p in range(16):
            grid[pl.ds((L + p) * PITCH, 2 * L), :] = grid[pl.ds(p * PITCH + 1, 2 * L), :]

    @pl.when(step == STEPS + BANDS - 1)
    def _():
        for slot, out_ref in enumerate(outs):
            start = starts_ref[slot]
            top = start // L
            shift = start % L
            for group in range(L // 16):
                p = shift + 16 * group
                wrapped = (p >= L).astype(jnp.int32)
                base = (p - L * wrapped) * PITCH + top + wrapped
                for plane in range(2):
                    for u in range(FS // L):
                        tile = grid[pl.ds(base + plane * L + u, 16, stride=PITCH), :]
                        out_ref[plane, u * L + 16 * group : u * L + 16 * group + 16, :] = tile.astype(jnp.bfloat16)


def columns_pass(x, g, tw, f, starts):
    targets = starts.shape[0]
    whole = lambda j, s: (0, 0)
    return pl.pallas_call(
        columns_body,
        name="columns_pass",
        grid_spec=pltpu.PrefetchScalarGridSpec(
            num_scalar_prefetch=1,
            grid=(STEPS + BANDS,),
            in_specs=[
                pl.BlockSpec((L, 2, 32, L), lambda j, s: (0, 0, jnp.minimum(j, STEPS - 1), 0)),
                pl.BlockSpec((2 * L, 2 * L), whole),
                pl.BlockSpec((1, 2, L, 32), lambda j, s: (jnp.minimum(j, STEPS - 1), 0, 0, 0)),
                pl.BlockSpec((2 * L, 2 * L), whole),
            ],
            out_specs=[pl.BlockSpec(memory_space=pltpu.VMEM)] * targets,
            scratch_shapes=[pltpu.VMEM((2 * L * 20, L), jnp.float32)] * 2
            + [pltpu.VMEM((16 * PITCH, L), jnp.float32)] * 2
            + [
                pltpu.VMEM((L, 2, L, L), jnp.bfloat16),
                pltpu.VMEM(((L + 16) * PITCH, L), jnp.float32),
            ],
        ),
        out_shape=[jax.ShapeDtypeStruct((2, FS, L), jnp.bfloat16)] * targets,
        compiler_params=params(46),
    )(starts, in_hbm(x), g, tw, f)


def facet_body_at(half, scal_ref, *refs):
    strips, down_ref, across_ref = refs[: REACH + 1], refs[REACH + 1], refs[REACH + 2]
    out_ref, ready, sems = refs[-3:]
    shift = scal_ref[0]
    owned = scal_ref[1].astype(jnp.float32)
    keep = lax.broadcasted_iota(jnp.int32, (16, L), 1) < L - shift
    back = lax.rem(L - shift, L)
    width = REACH * L
    block = L

    def store(k):
        rows = pl.ds(k * block, block)
        target = out_ref.at[0, :, rows, pl.ds(half * width, width)]
        return pltpu.make_async_copy(ready.at[:, rows, :], target, sems.at[k])

    def one(k, carry):
        for r in range(0, block, 16):
            rows = pl.ds(pl.multiple_of(k * block + r, 16), 16)
            down = jnp.broadcast_to(down_ref[rows], (16, L)) * owned
            for plane in range(2):
                last = pltpu.roll(strips[0][plane, rows].astype(jnp.float32), back, 1)
                for j in range(REACH):
                    this = pltpu.roll(strips[j + 1][plane, rows].astype(jnp.float32), back, 1)
                    weight = down * across_ref[:, j * L : (j + 1) * L]
                    tile = jnp.where(keep, last, this) * weight
                    ready[plane, rows, j * L : (j + 1) * L] = tile.astype(jnp.bfloat16)
                    last = this
        store(k).start()
        return carry

    lax.fori_loop(0, FS // block, one, 0)
    for k in range(FS // block):
        store(k).wait()


def facet_half(half, strips, scalars, before):
    taper = (0.25 + 0.75 * np.sin(math.pi * (np.arange(FS) + 0.5) / FS)).astype(np.float32)
    width = REACH * L
    vmem = pl.BlockSpec(memory_space=pltpu.VMEM)
    anywhere = pl.BlockSpec(memory_space=pl.ANY)
    args = [*strips, jnp.asarray(taper[:, None]), jnp.asarray(taper[None, half * width : (half + 1) * width])]
    extra = {}
    if before is not None:
        extra = dict(input_output_aliases={len(args) + 1: 0})
        args.append(before)
    return pl.pallas_call(
        partial(facet_body_at, half),
        name="facet",
        in_specs=[pl.BlockSpec(memory_space=pltpu.SMEM)]
        + [vmem] * (len(strips) + 2)
        + [anywhere] * (len(args) - len(strips) - 2),
        out_specs=anywhere,
        out_shape=pltpu.HBM((1, 2, FS, FS), jnp.bfloat16),
        scratch_shapes=[pltpu.VMEM((2, FS, width), jnp.bfloat16), pltpu.SemaphoreType.DMA((FS // L,))],
        compiler_params=params(16),
        **extra,
    )(scalars, *args)


def shifted(block, axis, distance):
    devices = range(lax.axis_size(axis))
    route = [((i - distance) % len(devices), i) for i in devices]
    return lax.ppermute(block, axis, route)


def shards(sky_image, facet_rows, facet_offsets, facet_owner):
    both = ("row", "col")
    devices = lax.axis_size(both)
    first_rows = real_form([(plane, 16 * c + a) for c in range(8) for plane in range(2) for a in range(16)])
    second_rows = real_form([(plane, b) for plane in range(2) for b in range(L)])
    first_cols = real_form([(plane, s) for s in range(L) for plane in range(2)])
    second_cols = real_form([(plane, i) for plane in range(2) for i in range(L)])
    turn = twiddles()
    turn_cols = turn.reshape(2, L, STEPS, L // STEPS).transpose(2, 0, 1, 3)

    my_index = lax.axis_index(both)
    targets = (my_index + jnp.arange(REACH, -REACH - 1, -1, dtype=jnp.int32)) % devices
    matches = (facet_owner[None, :] == targets[:, None]).astype(jnp.int32)
    owned = jnp.sum(matches, axis=1)
    starts = jnp.where(owned > 0, jnp.sum(matches * facet_rows[None, :], axis=1) - FS // 2, 0)
    offset = jnp.sum(matches[REACH] * facet_offsets)
    scalars = jnp.stack((offset, owned[REACH]))

    sent = pack(sky_image)
    strip = lax.all_to_all(sent, "col", split_axis=0, concat_axis=0, tiled=True)
    strip = strip.reshape(lax.axis_size("col"), L, 2, 16, L)
    done = rows_pass(strip, first_rows, second_rows, jnp.asarray(turn))
    columns = lax.all_to_all(done, both, split_axis=0, concat_axis=0, tiled=True)
    cut = columns_pass(columns, first_cols, jnp.asarray(turn_cols), second_cols, starts)
    strips = []
    for slot, distance in enumerate(range(REACH, -REACH - 1, -1)):
        strips.append(cut[slot] if distance == 0 else shifted(cut[slot], both, distance))
    facets = facet_half(0, strips[: REACH + 1], scalars, None)
    return facet_half(1, strips[REACH:], scalars, facets)


def solution(mesh):
    placed = (P(None, "row", "col"), P(), P(), P())
    return jax.shard_map(
        shards,
        mesh=mesh,
        in_specs=placed,
        out_specs=P(("row", "col"), None, None, None),
        check_vma=False,
    )
```

```python
import math
from functools import partial

import jax
import jax.numpy as jnp
import numpy as np
from jax import lax
from jax.experimental import pallas as pl
from jax.experimental.pallas import tpu as pltpu
from jax.sharding import PartitionSpec as P

N = 16384
FS = 1024
L = 128
REACH = 4
MIB = 1 << 20
PITCH = 2 * L + 4
ROW_GROUPS = 2


def dft_parts():
    k = np.arange(L)
    angles = (k[:, None] * k[None, :] % L) * (-2.0 * math.pi / L)
    scale = 1.0 / math.sqrt(L)
    return np.cos(angles) * scale, np.sin(angles) * scale


def twiddles():
    k = np.arange(L)
    angles = (k[:, None] * k[None, :] % N) * (-2.0 * math.pi / N)
    return np.stack((np.cos(angles), np.sin(angles))).astype(np.float32)


def real_form(order):
    re, im = dft_parts()
    plane = np.array([o[0] for o in order])
    index = np.array([o[1] for o in order])
    top = np.where(plane[None, :] == 0, re[:, index], -im[:, index])
    low = np.where(plane[None, :] == 0, im[:, index], re[:, index])
    return jnp.asarray(np.concatenate((top, low)), jnp.bfloat16)


def in_hbm(array):
    return pltpu.with_memory_space_constraint(array, pltpu.HBM)


def params(limit):
    return pltpu.CompilerParams(vmem_limit_bytes=limit * MIB)


PACK_ROWS = 64
AHEAD = 4


def pack_body(x_ref, out_ref, taken, given, scr, in_sems, out_sems):
    slices = x_ref.shape[1] // PACK_ROWS

    def fetch(k):
        return pltpu.make_async_copy(x_ref.at[:, pl.ds(k * PACK_ROWS, PACK_ROWS), :], taken.at[k], in_sems.at[k])

    def store(k):
        return pltpu.make_async_copy(given.at[k], out_ref.at[pl.ds(k * PACK_ROWS, PACK_ROWS)], out_sems.at[k])

    for k in range(AHEAD):
        fetch(k).start()

    def one(k, carry):
        fetch(k).wait()

        @pl.when(k + AHEAD < slices)
        def _():
            fetch(k + AHEAD).start()

        for plane in range(2):
            for a in range(16):
                scr[pl.ds((plane * 16 + a) * 68, PACK_ROWS), :] = taken[k, plane, :, a * L : (a + 1) * L].astype(
                    jnp.float32
                )
            for i in range(PACK_ROWS):
                given[k, i, plane] = scr[pl.ds(plane * 16 * 68 + i, 16, stride=68), :].astype(jnp.bfloat16)
        store(k).start()
        return carry

    lax.fori_loop(0, slices, one, 0)

    def drain(k, carry):
        store(k).wait()
        return carry

    lax.fori_loop(0, slices, drain, 0)


def pack(image):
    rows = image.shape[1]
    slices = rows // PACK_ROWS
    return pl.pallas_call(
        pack_body,
        name="pack",
        in_specs=[pl.BlockSpec(memory_space=pl.ANY)],
        out_specs=pl.BlockSpec(memory_space=pl.ANY),
        out_shape=pltpu.HBM((rows, 2, 16, L), jnp.bfloat16),
        scratch_shapes=[
            pltpu.VMEM((slices, 2, PACK_ROWS, 16 * L), jnp.bfloat16),
            pltpu.VMEM((slices, PACK_ROWS, 2, 16, L), jnp.bfloat16),
            pltpu.VMEM((2 * 16 * 68, L), jnp.float32),
            pltpu.SemaphoreType.DMA((slices,)),
            pltpu.SemaphoreType.DMA((slices,)),
        ],
        compiler_params=params(32),
    )(in_hbm(image))


def rows_body(x_ref, g_ref, h_ref, tw_ref, out_ref, scr):
    first = pl.program_id(0) * 16 * ROW_GROUPS
    for group in range(ROW_GROUPS):
        base = group * 16 * PITCH
        row = pl.multiple_of(first + group * 16, 16)
        for pair in range(8):
            data = jnp.concatenate([x_ref[:, row + 2 * pair + e].reshape(2 * L, L) for e in range(2)], axis=1)
            mixed = jnp.dot(g_ref[...], data, preferred_element_type=jnp.float32)
            turned = []
            for e in range(2):
                re = mixed[:L, e * L : (e + 1) * L]
                im = mixed[L:, e * L : (e + 1) * L]
                turned.append(
                    jnp.concatenate(
                        (
                            (re * tw_ref[0] - im * tw_ref[1]).astype(jnp.bfloat16),
                            (re * tw_ref[1] + im * tw_ref[0]).astype(jnp.bfloat16),
                        ),
                        axis=1,
                    )
                )
            section = jnp.concatenate(turned, axis=0)
            done = lax.dot_general(h_ref[...], section, (((1,), (1,)), ((), ())), preferred_element_type=jnp.float32)
            for e in range(2):
                scr[pl.ds(base + (2 * pair + e) * PITCH, 2 * L), :] = done[:, e * L : (e + 1) * L]
        for plane in range(2):
            for q in range(L):
                tile = scr[pl.ds(base + plane * L + q, 16, stride=PITCH), :]
                out_ref[q, plane, pl.ds(row, 16), :] = tile.astype(jnp.bfloat16)


def rows_pass(x, g, h, tw):
    _, rows = x.shape[:2]
    whole = lambda j: (0, 0)
    return pl.pallas_call(
        rows_body,
        name="rows_pass",
        grid=(rows // (16 * ROW_GROUPS),),
        in_specs=[
            pl.BlockSpec(memory_space=pltpu.VMEM),
            pl.BlockSpec((2 * L, 2 * L), whole),
            pl.BlockSpec((2 * L, 2 * L), whole),
            pl.BlockSpec((2, L, L), lambda j: (0, 0, 0)),
        ],
        out_specs=pl.BlockSpec(memory_space=pltpu.VMEM),
        out_shape=jax.ShapeDtypeStruct((L, 2, rows, L), jnp.bfloat16),
        scratch_shapes=[pltpu.VMEM((ROW_GROUPS * 16 * PITCH, L), jnp.float32)],
        compiler_params=params(24),
    )(x, g, h, tw)


STEPS = 4
BANDS = 4


def columns_body(starts_ref, x_ref, g_ref, tw_ref, f_ref, *refs):
    outs = refs[:-6]
    spreads, turns = refs[-6:-4], refs[-4:-2]
    section, grid = refs[-2:]
    step = pl.program_id(0)
    per = L // BANDS

    @pl.when(step < STEPS)
    def _():
        for group, (spread, turned) in enumerate(zip(spreads, turns)):
            rows = pl.ds(pl.multiple_of(step * 32 + group * 16, 16), 16)
            for k in range(2 * L):
                tile = x_ref[k // 2, k % 2, group * 16 : group * 16 + 16]
                spread[pl.ds(k * 20, 16), :] = tile.astype(jnp.float32)
            for pair in range(8):
                data = jnp.concatenate(
                    [spread[pl.ds(2 * pair + e, 2 * L, stride=20), :].astype(jnp.bfloat16) for e in range(2)], axis=1
                )
                mixed = jnp.dot(g_ref[...], data, preferred_element_type=jnp.float32)
                for e in range(2):
                    i = 2 * pair + e
                    re = mixed[:L, e * L : (e + 1) * L]
                    im = mixed[L:, e * L : (e + 1) * L]
                    at = group * 16 + i
                    t_re = jnp.broadcast_to(tw_ref[0, 0, :, at : at + 1], (L, L))
                    t_im = jnp.broadcast_to(tw_ref[0, 1, :, at : at + 1], (L, L))
                    turned[pl.ds(i * PITCH, L), :] = re * t_re - im * t_im
                    turned[pl.ds(i * PITCH + L, L), :] = re * t_im + im * t_re
            for plane in range(2):
                for p in range(L):
                    tile = turned[pl.ds(plane * L + p, 16, stride=PITCH), :]
                    section[p, plane, rows, :] = tile.astype(jnp.bfloat16)

    @pl.when(step == STEPS)
    def _():
        def second(k, carry):
            for pair in range(per // 2):
                p = k * per + 2 * pair
                data = jnp.concatenate([section[p + e].reshape(2 * L, L) for e in range(2)], axis=1)
                done = jnp.dot(f_ref[...], data, preferred_element_type=jnp.float32)
                for e in range(2):
                    grid[pl.ds((p + e) * PITCH, 2 * L), :] = done[:, e * L : (e + 1) * L]
            return carry

        lax.fori_loop(0, BANDS, second, 0)
        for p in range(16):
            grid[pl.ds((L + p) * PITCH, 2 * L), :] = grid[pl.ds(p * PITCH + 1, 2 * L), :]
        for slot, out_ref in enumerate(outs):
            start = starts_ref[slot]
            top = start // L
            shift = start % L
            for group in range(L // 16):
                p = shift + 16 * group
                wrapped = (p >= L).astype(jnp.int32)
                base = (p - L * wrapped) * PITCH + top + wrapped
                for plane in range(2):
                    for u in range(FS // L):
                        tile = grid[pl.ds(base + plane * L + u, 16, stride=PITCH), :]
                        out_ref[plane, u * L + 16 * group : u * L + 16 * group + 16, :] = tile.astype(jnp.bfloat16)


def columns_pass(x, g, tw, f, starts):
    targets = starts.shape[0]
    whole = lambda j, s: (0, 0)
    return pl.pallas_call(
        columns_body,
        name="columns_pass",
        grid_spec=pltpu.PrefetchScalarGridSpec(
            num_scalar_prefetch=1,
            grid=(STEPS + 1,),
            in_specs=[
                pl.BlockSpec((L, 2, 32, L), lambda j, s: (0, 0, jnp.minimum(j, STEPS - 1), 0)),
                pl.BlockSpec((2 * L, 2 * L), whole),
                pl.BlockSpec((1, 2, L, 32), lambda j, s: (jnp.minimum(j, STEPS - 1), 0, 0, 0)),
                pl.BlockSpec((2 * L, 2 * L), whole),
            ],
            out_specs=[pl.BlockSpec(memory_space=pltpu.VMEM)] * targets,
            scratch_shapes=[pltpu.VMEM((2 * L * 20, L), jnp.float32)] * 2
            + [pltpu.VMEM((16 * PITCH, L), jnp.float32)] * 2
            + [
                pltpu.VMEM((L, 2, L, L), jnp.bfloat16),
                pltpu.VMEM(((L + 16) * PITCH, L), jnp.float32),
            ],
        ),
        out_shape=[jax.ShapeDtypeStruct((2, FS, L), jnp.bfloat16)] * targets,
        compiler_params=params(46),
    )(starts, in_hbm(x), g, tw, f)


def facet_body_at(half, scal_ref, *refs):
    strips, down_ref, across_ref = refs[: REACH + 1], refs[REACH + 1], refs[REACH + 2]
    out_ref, ready, sems = refs[-3:]
    shift = scal_ref[0]
    owned = scal_ref[1].astype(jnp.float32)
    keep = lax.broadcasted_iota(jnp.int32, (16, L), 1) < L - shift
    back = lax.rem(L - shift, L)
    width = REACH * L
    block = L

    def store(k):
        rows = pl.ds(k * block, block)
        target = out_ref.at[0, :, rows, pl.ds(half * width, width)]
        return pltpu.make_async_copy(ready.at[:, rows, :], target, sems.at[k])

    def one(k, carry):
        for r in range(0, block, 16):
            rows = pl.ds(pl.multiple_of(k * block + r, 16), 16)
            down = jnp.broadcast_to(down_ref[rows], (16, L)) * owned
            for plane in range(2):
                last = pltpu.roll(strips[0][plane, rows].astype(jnp.float32), back, 1)
                for j in range(REACH):
                    this = pltpu.roll(strips[j + 1][plane, rows].astype(jnp.float32), back, 1)
                    weight = down * across_ref[:, j * L : (j + 1) * L]
                    tile = jnp.where(keep, last, this) * weight
                    ready[plane, rows, j * L : (j + 1) * L] = tile.astype(jnp.bfloat16)
                    last = this
        store(k).start()
        return carry

    lax.fori_loop(0, FS // block, one, 0)
    for k in range(FS // block):
        store(k).wait()


def facet_half(half, strips, scalars, before):
    taper = (0.25 + 0.75 * np.sin(math.pi * (np.arange(FS) + 0.5) / FS)).astype(np.float32)
    width = REACH * L
    vmem = pl.BlockSpec(memory_space=pltpu.VMEM)
    anywhere = pl.BlockSpec(memory_space=pl.ANY)
    args = [*strips, jnp.asarray(taper[:, None]), jnp.asarray(taper[None, half * width : (half + 1) * width])]
    extra = {}
    if before is not None:
        extra = dict(input_output_aliases={len(args) + 1: 0})
        args.append(before)
    return pl.pallas_call(
        partial(facet_body_at, half),
        name="facet",
        in_specs=[pl.BlockSpec(memory_space=pltpu.SMEM)]
        + [vmem] * (len(strips) + 2)
        + [anywhere] * (len(args) - len(strips) - 2),
        out_specs=anywhere,
        out_shape=pltpu.HBM((1, 2, FS, FS), jnp.bfloat16),
        scratch_shapes=[pltpu.VMEM((2, FS, width), jnp.bfloat16), pltpu.SemaphoreType.DMA((FS // L,))],
        compiler_params=params(16),
        **extra,
    )(scalars, *args)


def shifted(block, axis, distance):
    devices = range(lax.axis_size(axis))
    route = [((i - distance) % len(devices), i) for i in devices]
    return lax.ppermute(block, axis, route)


def shards(sky_image, facet_rows, facet_offsets, facet_owner):
    both = ("row", "col")
    devices = lax.axis_size(both)
    first_rows = real_form([(plane, 16 * c + a) for c in range(8) for plane in range(2) for a in range(16)])
    second_rows = real_form([(plane, b) for plane in range(2) for b in range(L)])
    first_cols = real_form([(plane, s) for s in range(L) for plane in range(2)])
    second_cols = real_form([(plane, i) for plane in range(2) for i in range(L)])
    turn = twiddles()
    turn_cols = turn.reshape(2, L, STEPS, L // STEPS).transpose(2, 0, 1, 3)

    my_index = lax.axis_index(both)
    targets = (my_index + jnp.arange(REACH, -REACH - 1, -1, dtype=jnp.int32)) % devices
    matches = (facet_owner[None, :] == targets[:, None]).astype(jnp.int32)
    owned = jnp.sum(matches, axis=1)
    starts = jnp.where(owned > 0, jnp.sum(matches * facet_rows[None, :], axis=1) - FS // 2, 0)
    offset = jnp.sum(matches[REACH] * facet_offsets)
    scalars = jnp.stack((offset, owned[REACH]))

    sent = pack(sky_image)
    sent, starts, scalars = lax.optimization_barrier((sent, starts, scalars))
    strip = lax.all_to_all(sent, "col", split_axis=0, concat_axis=0, tiled=True)
    strip = strip.reshape(lax.axis_size("col"), L, 2, 16, L)
    done = rows_pass(strip, first_rows, second_rows, jnp.asarray(turn))
    columns = lax.all_to_all(done, both, split_axis=0, concat_axis=0, tiled=True)
    cut = columns_pass(columns, first_cols, jnp.asarray(turn_cols), second_cols, starts)
    strips = []
    for slot, distance in enumerate(range(REACH, -REACH - 1, -1)):
        strips.append(cut[slot] if distance == 0 else shifted(cut[slot], both, distance))
    facets = facet_half(0, strips[: REACH + 1], scalars, None)
    return facet_half(1, strips[REACH:], scalars, facets)


def solution(mesh):
    placed = (P(None, "row", "col"), P(), P(), P())
    return jax.shard_map(
        shards,
        mesh=mesh,
        in_specs=placed,
        out_specs=P(("row", "col"), None, None, None),
        check_vma=False,
    )
```

```python
import math
from functools import partial

import jax
import jax.numpy as jnp
import numpy as np
from jax import lax
from jax.experimental import pallas as pl
from jax.experimental.pallas import tpu as pltpu
from jax.sharding import PartitionSpec as P

N = 16384
FS = 1024
L = 128
REACH = 4
MIB = 1 << 20
PITCH = 2 * L + 4
ROW_GROUPS = 2


def dft_parts():
    k = np.arange(L)
    angles = (k[:, None] * k[None, :] % L) * (-2.0 * math.pi / L)
    scale = 1.0 / math.sqrt(L)
    return np.cos(angles) * scale, np.sin(angles) * scale


def twiddles():
    k = np.arange(L)
    angles = (k[:, None] * k[None, :] % N) * (-2.0 * math.pi / N)
    return np.stack((np.cos(angles), np.sin(angles))).astype(np.float32)


def real_form(order):
    re, im = dft_parts()
    plane = np.array([o[0] for o in order])
    index = np.array([o[1] for o in order])
    top = np.where(plane[None, :] == 0, re[:, index], -im[:, index])
    low = np.where(plane[None, :] == 0, im[:, index], re[:, index])
    return jnp.asarray(np.concatenate((top, low)), jnp.bfloat16)


def in_hbm(array):
    return pltpu.with_memory_space_constraint(array, pltpu.HBM)


def params(limit):
    return pltpu.CompilerParams(vmem_limit_bytes=limit * MIB)


PACK_ROWS = 64
AHEAD = 4
OFFSET = 2 * REACH + 1
OWNED = 2 * REACH + 2


def pack_body(mine_ref, x_ref, rows_ref, offsets_ref, owner_ref, out_ref, table_ref, taken, given, scr, in_sems, out_sems, small_tables, small_sems):
    slices = x_ref.shape[1] // PACK_ROWS

    def fetch(k):
        return pltpu.make_async_copy(x_ref.at[:, pl.ds(k * PACK_ROWS, PACK_ROWS), :], taken.at[k], in_sems.at[k])

    def store(k):
        return pltpu.make_async_copy(given.at[k], out_ref.at[pl.ds(k * PACK_ROWS, PACK_ROWS)], out_sems.at[k])

    for k in range(AHEAD):
        fetch(k).start()

    def small(k, source):
        return pltpu.make_async_copy(source, small_tables.at[k], small_sems.at[k])

    sources = (rows_ref, offsets_ref, owner_ref)
    for k, source in enumerate(sources):
        small(k, source).start()

    def one(k, carry):
        fetch(k).wait()

        @pl.when(k + AHEAD < slices)
        def _():
            fetch(k + AHEAD).start()

        for plane in range(2):
            for a in range(16):
                scr[pl.ds((plane * 16 + a) * 68, PACK_ROWS), :] = taken[k, plane, :, a * L : (a + 1) * L].astype(
                    jnp.float32
                )
            for i in range(PACK_ROWS):
                given[k, i, plane] = scr[pl.ds(plane * 16 * 68 + i, 16, stride=68), :].astype(jnp.bfloat16)
        store(k).start()
        return carry

    lax.fori_loop(0, slices, one, 0)
    for k, source in enumerate(sources):
        small(k, source).wait()
    slot = lax.broadcasted_iota(jnp.int32, (16, L), 0)
    target = lax.rem(mine_ref[0] + REACH - jnp.where(slot <= 2 * REACH, slot, REACH) + L, L)
    match = small_tables[2] == target
    pick = jnp.where(slot <= 2 * REACH, small_tables[0] - FS // 2, jnp.where(slot == OFFSET, small_tables[1], 1))
    chosen = jnp.sum(jnp.where(match, pick, 0).astype(jnp.float32), axis=1, keepdims=True)
    table_ref[...] = jnp.broadcast_to(chosen, (16, L)).astype(jnp.int32)

    def drain(k, carry):
        store(k).wait()
        return carry

    lax.fori_loop(0, slices, drain, 0)


def pack(image, mine, facet_rows, facet_offsets, facet_owner):
    rows = image.shape[1]
    slices = rows // PACK_ROWS
    vmem = pl.BlockSpec(memory_space=pltpu.VMEM)
    return pl.pallas_call(
        pack_body,
        name="pack",
        in_specs=[pl.BlockSpec(memory_space=pltpu.SMEM), *[pl.BlockSpec(memory_space=pl.ANY)] * 4],
        out_specs=[pl.BlockSpec(memory_space=pl.ANY), vmem],
        out_shape=[
            pltpu.HBM((rows, 2, 16, L), jnp.bfloat16),
            jax.ShapeDtypeStruct((16, L), jnp.int32),
        ],
        scratch_shapes=[
            pltpu.VMEM((slices, 2, PACK_ROWS, 16 * L), jnp.bfloat16),
            pltpu.VMEM((slices, PACK_ROWS, 2, 16, L), jnp.bfloat16),
            pltpu.VMEM((2 * 16 * 68, L), jnp.float32),
            pltpu.SemaphoreType.DMA((slices,)),
            pltpu.SemaphoreType.DMA((slices,)),
            pltpu.VMEM((3, 1, L), jnp.int32),
            pltpu.SemaphoreType.DMA((3,)),
        ],
        compiler_params=params(32),
    )(mine, in_hbm(image), *(in_hbm(t.reshape(1, L)) for t in (facet_rows, facet_offsets, facet_owner)))


def rows_body(x_ref, g_ref, h_ref, tw_ref, out_ref, scr):
    first = pl.program_id(0) * 16 * ROW_GROUPS
    for group in range(ROW_GROUPS):
        base = group * 16 * PITCH
        row = pl.multiple_of(first + group * 16, 16)
        for pair in range(8):
            data = jnp.concatenate([x_ref[:, row + 2 * pair + e].reshape(2 * L, L) for e in range(2)], axis=1)
            mixed = jnp.dot(g_ref[...], data, preferred_element_type=jnp.float32)
            turned = []
            for e in range(2):
                re = mixed[:L, e * L : (e + 1) * L]
                im = mixed[L:, e * L : (e + 1) * L]
                turned.append(
                    jnp.concatenate(
                        (
                            (re * tw_ref[0] - im * tw_ref[1]).astype(jnp.bfloat16),
                            (re * tw_ref[1] + im * tw_ref[0]).astype(jnp.bfloat16),
                        ),
                        axis=1,
                    )
                )
            section = jnp.concatenate(turned, axis=0)
            done = lax.dot_general(h_ref[...], section, (((1,), (1,)), ((), ())), preferred_element_type=jnp.float32)
            for e in range(2):
                scr[pl.ds(base + (2 * pair + e) * PITCH, 2 * L), :] = done[:, e * L : (e + 1) * L]
        for plane in range(2):
            for q in range(L):
                tile = scr[pl.ds(base + plane * L + q, 16, stride=PITCH), :]
                out_ref[q, plane, pl.ds(row, 16), :] = tile.astype(jnp.bfloat16)


def rows_pass(x, g, h, tw):
    _, rows = x.shape[:2]
    whole = lambda j: (0, 0)
    return pl.pallas_call(
        rows_body,
        name="rows_pass",
        grid=(rows // (16 * ROW_GROUPS),),
        in_specs=[
            pl.BlockSpec(memory_space=pltpu.VMEM),
            pl.BlockSpec((2 * L, 2 * L), whole),
            pl.BlockSpec((2 * L, 2 * L), whole),
            pl.BlockSpec((2, L, L), lambda j: (0, 0, 0)),
        ],
        out_specs=pl.BlockSpec(memory_space=pltpu.VMEM),
        out_shape=jax.ShapeDtypeStruct((L, 2, rows, L), jnp.bfloat16),
        scratch_shapes=[pltpu.VMEM((ROW_GROUPS * 16 * PITCH, L), jnp.float32)],
        compiler_params=params(24),
    )(x, g, h, tw)


STEPS = 4
BANDS = 4


def columns_body(starts_ref, x_ref, g_ref, tw_ref, f_ref, *refs):
    outs = refs[:-6]
    spreads, turns = refs[-6:-4], refs[-4:-2]
    section, grid = refs[-2:]
    step = pl.program_id(0)
    per = L // BANDS

    @pl.when(step < STEPS)
    def _():
        for group, (spread, turned) in enumerate(zip(spreads, turns)):
            rows = pl.ds(pl.multiple_of(step * 32 + group * 16, 16), 16)
            for k in range(2 * L):
                tile = x_ref[k // 2, k % 2, group * 16 : group * 16 + 16]
                spread[pl.ds(k * 20, 16), :] = tile.astype(jnp.float32)
            for pair in range(8):
                data = jnp.concatenate(
                    [spread[pl.ds(2 * pair + e, 2 * L, stride=20), :].astype(jnp.bfloat16) for e in range(2)], axis=1
                )
                mixed = jnp.dot(g_ref[...], data, preferred_element_type=jnp.float32)
                for e in range(2):
                    i = 2 * pair + e
                    re = mixed[:L, e * L : (e + 1) * L]
                    im = mixed[L:, e * L : (e + 1) * L]
                    at = group * 16 + i
                    t_re = jnp.broadcast_to(tw_ref[0, 0, :, at : at + 1], (L, L))
                    t_im = jnp.broadcast_to(tw_ref[0, 1, :, at : at + 1], (L, L))
                    turned[pl.ds(i * PITCH, L), :] = re * t_re - im * t_im
                    turned[pl.ds(i * PITCH + L, L), :] = re * t_im + im * t_re
            for plane in range(2):
                for p in range(L):
                    tile = turned[pl.ds(plane * L + p, 16, stride=PITCH), :]
                    section[p, plane, rows, :] = tile.astype(jnp.bfloat16)

    @pl.when(step == STEPS)
    def _():
        def second(k, carry):
            for pair in range(per // 2):
                p = k * per + 2 * pair
                data = jnp.concatenate([section[p + e].reshape(2 * L, L) for e in range(2)], axis=1)
                done = jnp.dot(f_ref[...], data, preferred_element_type=jnp.float32)
                for e in range(2):
                    grid[pl.ds((p + e) * PITCH, 2 * L), :] = done[:, e * L : (e + 1) * L]
            return carry

        lax.fori_loop(0, BANDS, second, 0)
        for p in range(16):
            grid[pl.ds((L + p) * PITCH, 2 * L), :] = grid[pl.ds(p * PITCH + 1, 2 * L), :]
        for slot, out_ref in enumerate(outs):
            start = starts_ref[slot, 0]
            top = start // L
            shift = start % L
            for group in range(L // 16):
                p = shift + 16 * group
                wrapped = (p >= L).astype(jnp.int32)
                base = (p - L * wrapped) * PITCH + top + wrapped
                for plane in range(2):
                    for u in range(FS // L):
                        tile = grid[pl.ds(base + plane * L + u, 16, stride=PITCH), :]
                        out_ref[plane, u * L + 16 * group : u * L + 16 * group + 16, :] = tile.astype(jnp.bfloat16)


def columns_pass(x, g, tw, f, starts):
    targets = 2 * REACH + 1
    whole = lambda j, s: (0, 0)
    return pl.pallas_call(
        columns_body,
        name="columns_pass",
        grid_spec=pltpu.PrefetchScalarGridSpec(
            num_scalar_prefetch=1,
            grid=(STEPS + 1,),
            in_specs=[
                pl.BlockSpec((L, 2, 32, L), lambda j, s: (0, 0, jnp.minimum(j, STEPS - 1), 0)),
                pl.BlockSpec((2 * L, 2 * L), whole),
                pl.BlockSpec((1, 2, L, 32), lambda j, s: (jnp.minimum(j, STEPS - 1), 0, 0, 0)),
                pl.BlockSpec((2 * L, 2 * L), whole),
            ],
            out_specs=[pl.BlockSpec(memory_space=pltpu.VMEM)] * targets,
            scratch_shapes=[pltpu.VMEM((2 * L * 20, L), jnp.float32)] * 2
            + [pltpu.VMEM((16 * PITCH, L), jnp.float32)] * 2
            + [
                pltpu.VMEM((L, 2, L, L), jnp.bfloat16),
                pltpu.VMEM(((L + 16) * PITCH, L), jnp.float32),
            ],
        ),
        out_shape=[jax.ShapeDtypeStruct((2, FS, L), jnp.bfloat16)] * targets,
        compiler_params=params(46),
    )(starts, in_hbm(x), g, tw, f)


def facet_body_at(half, scal_ref, *refs):
    strips, down_ref, across_ref = refs[: REACH + 1], refs[REACH + 1], refs[REACH + 2]
    out_ref, ready, sems = refs[-3:]
    shift = scal_ref[OFFSET, 0]
    owned = scal_ref[OWNED, 0].astype(jnp.float32)
    keep = lax.broadcasted_iota(jnp.int32, (16, L), 1) < L - shift
    back = lax.rem(L - shift, L)
    width = REACH * L
    block = L

    def store(k):
        rows = pl.ds(k * block, block)
        target = out_ref.at[0, :, rows, pl.ds(half * width, width)]
        return pltpu.make_async_copy(ready.at[:, rows, :], target, sems.at[k])

    def one(k, carry):
        for r in range(0, block, 16):
            rows = pl.ds(pl.multiple_of(k * block + r, 16), 16)
            down = jnp.broadcast_to(down_ref[rows], (16, L)) * owned
            for plane in range(2):
                last = pltpu.roll(strips[0][plane, rows].astype(jnp.float32), back, 1)
                for j in range(REACH):
                    this = pltpu.roll(strips[j + 1][plane, rows].astype(jnp.float32), back, 1)
                    weight = down * across_ref[:, j * L : (j + 1) * L]
                    tile = jnp.where(keep, last, this) * weight
                    ready[plane, rows, j * L : (j + 1) * L] = tile.astype(jnp.bfloat16)
                    last = this
        store(k).start()
        return carry

    lax.fori_loop(0, FS // block, one, 0)
    for k in range(FS // block):
        store(k).wait()


def facet_half(half, strips, scalars, before):
    taper = (0.25 + 0.75 * np.sin(math.pi * (np.arange(FS) + 0.5) / FS)).astype(np.float32)
    width = REACH * L
    vmem = pl.BlockSpec(memory_space=pltpu.VMEM)
    anywhere = pl.BlockSpec(memory_space=pl.ANY)
    args = [*strips, jnp.asarray(taper[:, None]), jnp.asarray(taper[None, half * width : (half + 1) * width])]
    extra = {}
    if before is not None:
        extra = dict(input_output_aliases={len(args) + 1: 0})
        args.append(before)
    return pl.pallas_call(
        partial(facet_body_at, half),
        name="facet",
        in_specs=[pl.BlockSpec(memory_space=pltpu.SMEM)]
        + [vmem] * (len(strips) + 2)
        + [anywhere] * (len(args) - len(strips) - 2),
        out_specs=anywhere,
        out_shape=pltpu.HBM((1, 2, FS, FS), jnp.bfloat16),
        scratch_shapes=[pltpu.VMEM((2, FS, width), jnp.bfloat16), pltpu.SemaphoreType.DMA((FS // L,))],
        compiler_params=params(16),
        **extra,
    )(scalars, *args)


def shifted(block, axis, distance):
    devices = range(lax.axis_size(axis))
    route = [((i - distance) % len(devices), i) for i in devices]
    return lax.ppermute(block, axis, route)


def shards(sky_image, facet_rows, facet_offsets, facet_owner):
    both = ("row", "col")
    first_rows = real_form([(plane, 16 * c + a) for c in range(8) for plane in range(2) for a in range(16)])
    second_rows = real_form([(plane, b) for plane in range(2) for b in range(L)])
    first_cols = real_form([(plane, s) for s in range(L) for plane in range(2)])
    second_cols = real_form([(plane, i) for plane in range(2) for i in range(L)])
    turn = twiddles()
    turn_cols = turn.reshape(2, L, STEPS, L // STEPS).transpose(2, 0, 1, 3)

    my_index = lax.axis_index(both)
    sent, table = pack(sky_image, my_index.astype(jnp.int32)[None], facet_rows, facet_offsets, facet_owner)
    strip = lax.all_to_all(sent, "col", split_axis=0, concat_axis=0, tiled=True)
    strip = strip.reshape(lax.axis_size("col"), L, 2, 16, L)
    done = rows_pass(strip, first_rows, second_rows, jnp.asarray(turn))
    columns = lax.all_to_all(done, both, split_axis=0, concat_axis=0, tiled=True)
    cut = columns_pass(columns, first_cols, jnp.asarray(turn_cols), second_cols, table)
    strips = []
    for slot, distance in enumerate(range(REACH, -REACH - 1, -1)):
        strips.append(cut[slot] if distance == 0 else shifted(cut[slot], both, distance))
    facets = facet_half(0, strips[: REACH + 1], table, None)
    return facet_half(1, strips[REACH:], table, facets)


def solution(mesh):
    placed = (P(None, "row", "col"), P(), P(), P())
    return jax.shard_map(
        shards,
        mesh=mesh,
        in_specs=placed,
        out_specs=P(("row", "col"), None, None, None),
        check_vma=False,
    )
```

```python
import math
from functools import partial

import jax
import jax.numpy as jnp
import numpy as np
from jax import lax
from jax.experimental import pallas as pl
from jax.experimental.pallas import tpu as pltpu
from jax.sharding import PartitionSpec as P

N = 16384
FS = 1024
L = 128
REACH = 4
MIB = 1 << 20
PITCH = 2 * L + 4
ROW_GROUPS = 4


def dft_parts():
    k = np.arange(L)
    angles = (k[:, None] * k[None, :] % L) * (-2.0 * math.pi / L)
    scale = 1.0 / math.sqrt(L)
    return np.cos(angles) * scale, np.sin(angles) * scale


def twiddles():
    k = np.arange(L)
    angles = (k[:, None] * k[None, :] % N) * (-2.0 * math.pi / N)
    return np.stack((np.cos(angles), np.sin(angles))).astype(np.float32)


def real_form(order):
    re, im = dft_parts()
    plane = np.array([o[0] for o in order])
    index = np.array([o[1] for o in order])
    top = np.where(plane[None, :] == 0, re[:, index], -im[:, index])
    low = np.where(plane[None, :] == 0, im[:, index], re[:, index])
    return jnp.asarray(np.concatenate((top, low)), jnp.bfloat16)


def in_hbm(array):
    return pltpu.with_memory_space_constraint(array, pltpu.HBM)


def params(limit):
    return pltpu.CompilerParams(vmem_limit_bytes=limit * MIB)


PACK_ROWS = 64
AHEAD = 4
OFFSET = 2 * REACH + 1
OWNED = 2 * REACH + 2


def pack_body(mine_ref, x_ref, rows_ref, offsets_ref, owner_ref, out_ref, table_ref, taken, scr, in_sems, small_tables, small_sems):
    slices = x_ref.shape[1] // PACK_ROWS

    def fetch(k):
        return pltpu.make_async_copy(x_ref.at[:, pl.ds(k * PACK_ROWS, PACK_ROWS), :], taken.at[k], in_sems.at[k])

    for k in range(AHEAD):
        fetch(k).start()

    def small(k, source):
        return pltpu.make_async_copy(source, small_tables.at[k], small_sems.at[k])

    sources = (rows_ref, offsets_ref, owner_ref)
    for k, source in enumerate(sources):
        small(k, source).start()

    def one(k, carry):
        fetch(k).wait()

        @pl.when(k + AHEAD < slices)
        def _():
            fetch(k + AHEAD).start()

        for plane in range(2):
            for a in range(16):
                scr[pl.ds((plane * 16 + a) * 68, PACK_ROWS), :] = taken[k, plane, :, a * L : (a + 1) * L].astype(
                    jnp.float32
                )
            for i in range(PACK_ROWS):
                out_ref[k * PACK_ROWS + i, plane] = scr[pl.ds(plane * 16 * 68 + i, 16, stride=68), :].astype(jnp.bfloat16)
        return carry

    lax.fori_loop(0, slices, one, 0)
    for k, source in enumerate(sources):
        small(k, source).wait()
    slot = lax.broadcasted_iota(jnp.int32, (16, L), 0)
    target = lax.rem(mine_ref[0] + REACH - jnp.where(slot <= 2 * REACH, slot, REACH) + L, L)
    match = small_tables[2] == target
    pick = jnp.where(slot <= 2 * REACH, small_tables[0] - FS // 2, jnp.where(slot == OFFSET, small_tables[1], 1))
    chosen = jnp.sum(jnp.where(match, pick, 0).astype(jnp.float32), axis=1, keepdims=True)
    table_ref[...] = jnp.broadcast_to(chosen, (16, L)).astype(jnp.int32)


def pack(image, mine, facet_rows, facet_offsets, facet_owner):
    rows = image.shape[1]
    slices = rows // PACK_ROWS
    vmem = pl.BlockSpec(memory_space=pltpu.VMEM)
    return pl.pallas_call(
        pack_body,
        name="pack",
        in_specs=[pl.BlockSpec(memory_space=pltpu.SMEM), *[pl.BlockSpec(memory_space=pl.ANY)] * 4],
        out_specs=[vmem, vmem],
        out_shape=[
            jax.ShapeDtypeStruct((rows, 2, 16, L), jnp.bfloat16),
            jax.ShapeDtypeStruct((16, L), jnp.int32),
        ],
        scratch_shapes=[
            pltpu.VMEM((slices, 2, PACK_ROWS, 16 * L), jnp.bfloat16),
            pltpu.VMEM((2 * 16 * 68, L), jnp.float32),
            pltpu.SemaphoreType.DMA((slices,)),
            pltpu.VMEM((3, 1, L), jnp.int32),
            pltpu.SemaphoreType.DMA((3,)),
        ],
        compiler_params=params(16),
    )(mine, in_hbm(image), *(in_hbm(t.reshape(1, L)) for t in (facet_rows, facet_offsets, facet_owner)))


def rows_body(x_ref, g_ref, h_ref, tw_ref, out_ref, scr):
    first = pl.program_id(0) * 16 * ROW_GROUPS
    for group in range(ROW_GROUPS):
        base = group * 16 * PITCH
        row = pl.multiple_of(first + group * 16, 16)
        for pair in range(8):
            data = jnp.concatenate([x_ref[:, row + 2 * pair + e].reshape(2 * L, L) for e in range(2)], axis=1)
            mixed = jnp.dot(g_ref[...], data, preferred_element_type=jnp.float32)
            turned = []
            for e in range(2):
                re = mixed[:L, e * L : (e + 1) * L]
                im = mixed[L:, e * L : (e + 1) * L]
                turned.append(
                    jnp.concatenate(
                        (
                            (re * tw_ref[0] - im * tw_ref[1]).astype(jnp.bfloat16),
                            (re * tw_ref[1] + im * tw_ref[0]).astype(jnp.bfloat16),
                        ),
                        axis=1,
                    )
                )
            section = jnp.concatenate(turned, axis=0)
            done = lax.dot_general(h_ref[...], section, (((1,), (1,)), ((), ())), preferred_element_type=jnp.float32)
            for e in range(2):
                scr[pl.ds(base + (2 * pair + e) * PITCH, 2 * L), :] = done[:, e * L : (e + 1) * L]
        for plane in range(2):
            for q in range(L):
                tile = scr[pl.ds(base + plane * L + q, 16, stride=PITCH), :]
                out_ref[q, plane, pl.ds(row, 16), :] = tile.astype(jnp.bfloat16)


def rows_pass(x, g, h, tw):
    _, rows = x.shape[:2]
    whole = lambda j: (0, 0)
    return pl.pallas_call(
        rows_body,
        name="rows_pass",
        grid=(rows // (16 * ROW_GROUPS),),
        in_specs=[
            pl.BlockSpec(memory_space=pltpu.VMEM),
            pl.BlockSpec((2 * L, 2 * L), whole),
            pl.BlockSpec((2 * L, 2 * L), whole),
            pl.BlockSpec((2, L, L), lambda j: (0, 0, 0)),
        ],
        out_specs=pl.BlockSpec(memory_space=pltpu.VMEM),
        out_shape=jax.ShapeDtypeStruct((L, 2, rows, L), jnp.bfloat16),
        scratch_shapes=[pltpu.VMEM((ROW_GROUPS * 16 * PITCH, L), jnp.float32)],
        compiler_params=params(24),
    )(x, g, h, tw)


STEPS = 4
BANDS = 2


def columns_body(starts_ref, x_ref, g_ref, tw_ref, f_ref, *refs):
    outs = refs[:-6]
    spreads, turns = refs[-6:-4], refs[-4:-2]
    section, grid = refs[-2:]
    step = pl.program_id(0)
    per = L // BANDS

    @pl.when(step < STEPS)
    def _():
        for group, (spread, turned) in enumerate(zip(spreads, turns)):
            rows = pl.ds(pl.multiple_of(step * 32 + group * 16, 16), 16)
            for k in range(2 * L):
                tile = x_ref[k // 2, k % 2, group * 16 : group * 16 + 16]
                spread[pl.ds(k * 20, 16), :] = tile.astype(jnp.float32)
            for pair in range(8):
                data = jnp.concatenate(
                    [spread[pl.ds(2 * pair + e, 2 * L, stride=20), :].astype(jnp.bfloat16) for e in range(2)], axis=1
                )
                mixed = jnp.dot(g_ref[...], data, preferred_element_type=jnp.float32)
                for e in range(2):
                    i = 2 * pair + e
                    re = mixed[:L, e * L : (e + 1) * L]
                    im = mixed[L:, e * L : (e + 1) * L]
                    at = group * 16 + i
                    t_re = jnp.broadcast_to(tw_ref[0, 0, :, at : at + 1], (L, L))
                    t_im = jnp.broadcast_to(tw_ref[0, 1, :, at : at + 1], (L, L))
                    turned[pl.ds(i * PITCH, L), :] = re * t_re - im * t_im
                    turned[pl.ds(i * PITCH + L, L), :] = re * t_im + im * t_re
            for plane in range(2):
                for p in range(L):
                    tile = turned[pl.ds(plane * L + p, 16, stride=PITCH), :]
                    section[p, plane, rows, :] = tile.astype(jnp.bfloat16)

    @pl.when(step == STEPS)
    def _():
        def second(k, carry):
            for pair in range(per // 2):
                p = k * per + 2 * pair
                data = jnp.concatenate([section[p + e].reshape(2 * L, L) for e in range(2)], axis=1)
                done = jnp.dot(f_ref[...], data, preferred_element_type=jnp.float32)
                for e in range(2):
                    grid[pl.ds((p + e) * PITCH, 2 * L), :] = done[:, e * L : (e + 1) * L]
            return carry

        lax.fori_loop(0, BANDS, second, 0)
        for p in range(16):
            grid[pl.ds((L + p) * PITCH, 2 * L), :] = grid[pl.ds(p * PITCH + 1, 2 * L), :]
        for slot, out_ref in enumerate(outs):
            start = starts_ref[slot, 0]
            top = start // L
            shift = start % L
            for group in range(L // 16):
                p = shift + 16 * group
                wrapped = (p >= L).astype(jnp.int32)
                base = (p - L * wrapped) * PITCH + top + wrapped
                for plane in range(2):
                    for u in range(FS // L):
                        tile = grid[pl.ds(base + plane * L + u, 16, stride=PITCH), :]
                        out_ref[plane, u * L + 16 * group : u * L + 16 * group + 16, :] = tile.astype(jnp.bfloat16)


def columns_pass(x, g, tw, f, starts):
    targets = 2 * REACH + 1
    whole = lambda j, s: (0, 0)
    return pl.pallas_call(
        columns_body,
        name="columns_pass",
        grid_spec=pltpu.PrefetchScalarGridSpec(
            num_scalar_prefetch=1,
            grid=(STEPS + 1,),
            in_specs=[
                pl.BlockSpec((L, 2, 32, L), lambda j, s: (0, 0, jnp.minimum(j, STEPS - 1), 0)),
                pl.BlockSpec((2 * L, 2 * L), whole),
                pl.BlockSpec((1, 2, L, 32), lambda j, s: (jnp.minimum(j, STEPS - 1), 0, 0, 0)),
                pl.BlockSpec((2 * L, 2 * L), whole),
            ],
            out_specs=[pl.BlockSpec(memory_space=pltpu.VMEM)] * targets,
            scratch_shapes=[pltpu.VMEM((2 * L * 20, L), jnp.float32)] * 2
            + [pltpu.VMEM((16 * PITCH, L), jnp.float32)] * 2
            + [
                pltpu.VMEM((L, 2, L, L), jnp.bfloat16),
                pltpu.VMEM(((L + 16) * PITCH, L), jnp.float32),
            ],
        ),
        out_shape=[jax.ShapeDtypeStruct((2, FS, L), jnp.bfloat16)] * targets,
        compiler_params=params(46),
    )(starts, in_hbm(x), g, tw, f)


def facet_body_at(half, scal_ref, *refs):
    strips, down_ref, across_ref = refs[: REACH + 1], refs[REACH + 1], refs[REACH + 2]
    out_ref, ready, sems = refs[-3:]
    shift = scal_ref[OFFSET, 0]
    owned = scal_ref[OWNED, 0].astype(jnp.float32)
    keep = lax.broadcasted_iota(jnp.int32, (16, L), 1) < L - shift
    back = lax.rem(L - shift, L)
    width = REACH * L
    block = L

    def store(k):
        rows = pl.ds(k * block, block)
        target = out_ref.at[0, :, rows, pl.ds(half * width, width)]
        return pltpu.make_async_copy(ready.at[:, rows, :], target, sems.at[k])

    def one(k, carry):
        for r in range(0, block, 16):
            rows = pl.ds(pl.multiple_of(k * block + r, 16), 16)
            down = jnp.broadcast_to(down_ref[rows], (16, L)) * owned
            for plane in range(2):
                last = pltpu.roll(strips[0][plane, rows].astype(jnp.float32), back, 1)
                for j in range(REACH):
                    this = pltpu.roll(strips[j + 1][plane, rows].astype(jnp.float32), back, 1)
                    weight = down * across_ref[:, j * L : (j + 1) * L]
                    tile = jnp.where(keep, last, this) * weight
                    ready[plane, rows, j * L : (j + 1) * L] = tile.astype(jnp.bfloat16)
                    last = this
        store(k).start()
        return carry

    lax.fori_loop(0, FS // block, one, 0)
    for k in range(FS // block):
        store(k).wait()


def facet_half(half, strips, scalars, before):
    taper = (0.25 + 0.75 * np.sin(math.pi * (np.arange(FS) + 0.5) / FS)).astype(np.float32)
    width = REACH * L
    vmem = pl.BlockSpec(memory_space=pltpu.VMEM)
    anywhere = pl.BlockSpec(memory_space=pl.ANY)
    args = [*strips, jnp.asarray(taper[:, None]), jnp.asarray(taper[None, half * width : (half + 1) * width])]
    extra = {}
    if before is not None:
        extra = dict(input_output_aliases={len(args) + 1: 0})
        args.append(before)
    return pl.pallas_call(
        partial(facet_body_at, half),
        name="facet",
        in_specs=[pl.BlockSpec(memory_space=pltpu.SMEM)]
        + [vmem] * (len(strips) + 2)
        + [anywhere] * (len(args) - len(strips) - 2),
        out_specs=anywhere,
        out_shape=pltpu.HBM((1, 2, FS, FS), jnp.bfloat16),
        scratch_shapes=[pltpu.VMEM((2, FS, width), jnp.bfloat16), pltpu.SemaphoreType.DMA((FS // L,))],
        compiler_params=params(16),
        **extra,
    )(scalars, *args)


def shifted(block, axis, distance):
    devices = range(lax.axis_size(axis))
    route = [((i - distance) % len(devices), i) for i in devices]
    return lax.ppermute(block, axis, route)


def shards(sky_image, facet_rows, facet_offsets, facet_owner):
    both = ("row", "col")
    first_rows = real_form([(plane, 16 * c + a) for c in range(8) for plane in range(2) for a in range(16)])
    second_rows = real_form([(plane, b) for plane in range(2) for b in range(L)])
    first_cols = real_form([(plane, s) for s in range(L) for plane in range(2)])
    second_cols = real_form([(plane, i) for plane in range(2) for i in range(L)])
    turn = twiddles()
    turn_cols = turn.reshape(2, L, STEPS, L // STEPS).transpose(2, 0, 1, 3)

    my_index = lax.axis_index(both)
    sent, table = pack(sky_image, my_index.astype(jnp.int32)[None], facet_rows, facet_offsets, facet_owner)
    strip = lax.all_to_all(sent, "col", split_axis=0, concat_axis=0, tiled=True)
    strip = strip.reshape(lax.axis_size("col"), L, 2, 16, L)
    done = rows_pass(strip, first_rows, second_rows, jnp.asarray(turn))
    columns = lax.all_to_all(done, both, split_axis=0, concat_axis=0, tiled=True)
    cut = columns_pass(columns, first_cols, jnp.asarray(turn_cols), second_cols, table)
    strips = []
    for slot, distance in enumerate(range(REACH, -REACH - 1, -1)):
        strips.append(cut[slot] if distance == 0 else shifted(cut[slot], both, distance))
    facets = facet_half(0, strips[: REACH + 1], table, None)
    return facet_half(1, strips[REACH:], table, facets)


def solution(mesh):
    placed = (P(None, "row", "col"), P(), P(), P())
    return jax.shard_map(
        shards,
        mesh=mesh,
        in_specs=placed,
        out_specs=P(("row", "col"), None, None, None),
        check_vma=False,
    )
```
